32 devices in a mesh: groups: 2 (over x), view: 16 (over z, y, core).
Axes of the slice: x: 2, y: 2, z: 4, core: 2. Of those that a mesh axis runs over, the one named last changes fastest.
Arguments:
- materials: float32 [3, 64, 256, 512], P(None, ('groups', 'view')), parts along dimension 1, as said below
- column_profile: bfloat16 [2, 512, 1280], replicated, as said below
- row_profile: bfloat16 [2, 256, 1280], replicated, as said below
- start_block: int32 [32], P(('groups', 'view')), parts along dimension 0, may hold values from 0 to 30, as said below
- block_count: int32 [32], P(('groups', 'view')), parts along dimension 0, may hold values from 1 to 4, as said below
- tile_ids: int32 [32, 4], P(('groups', 'view')), parts along dimension 0, may hold values from 0 to 1
- photon_counts: int32 [32, 8, 4, 1280], P(('groups', 'view')), parts along dimension 0, may hold values from 0 to 3199
- spectrum: float32 [8, 16], replicated, may hold values from 20 to 200
- attenuation: float32 [16, 3], replicated, may hold values from 0.05 to 0.5
- step_size: float32 [3], replicated, may hold values from 0.002 to 0.01
Outputs:
- updated: float32 [3, 64, 256, 512], P(None, ('groups', 'view')), parts along dimension 1
The draws below stay inside these ranges and needn't reach their ends.
There are 2 independent parts, one for each index of `groups`. The reference program is written for one: setup_inputs(seed, part) draws one part's arguments, and reference() takes and returns one part's arrays. A program takes and returns all parts, laid end to end along the dimension named above; an argument that names none is the same for every part. Nothing has to cross between parts.
Inputs may be any that keep to these rules, and one draw needn't show every extreme that they name: `start_block`: every slice of a view's window lies among the 2 slices of the device that holds the view (view v belongs to device v) and the 2 slices on either side; the window ends at or before slice 32 - 1. `block_count`: windows of views are ragged; some view of every scan covers 4 slices. `column_profile`: entries are non-negative and below 1. `row_profile`: entries are non-negative and below 1. `materials`: entries lie between 0 and 1.
All inputs are finite; a program needn't handle non-finite values.
Results may differ from the reference program's by a relative error of at most 0.00057.
Values may be sent and summed in bfloat16 or wider, within the bound.
A program may use at most 64 MiB of HBM per device.

```python
import math
import jax
import jax.numpy as jnp
from jax import lax

M = 3
E = 8
K = 16
PIX = 1280
SX = 512
SY = 256
WMAX = 4
VPD = 1
BLK_DEV = 2
NT = 2
ITERS = 2
DROWS = 4
NB = 32
VIEWS = 16
N_VIEW = 16


def window_pair(key):
    key_offset, key_count = jax.random.split(jax.random.fold_in(key, 4242))
    views = jnp.arange(VIEWS).astype(jnp.int32)
    owner = views // VPD
    offset = jax.random.randint(key_offset, (VIEWS,), -BLK_DEV, 2 * BLK_DEV - WMAX + 1).astype(jnp.int32)
    number = jax.random.randint(key_count, (VIEWS,), 1, WMAX + 1).astype(jnp.int32)
    number = jnp.where(views == 2 * VPD, 1, number)
    reach_down = (views == VIEWS - 1) | (views == VPD)
    reach_up = (views == 0) | (views == (N_VIEW - 1) * VPD - 1)
    offset = jnp.where(reach_down, -BLK_DEV, offset)
    offset = jnp.where(reach_up, 2 * BLK_DEV - WMAX, offset)
    number = jnp.where(reach_down | reach_up, WMAX, number)
    first = jnp.maximum(owner * BLK_DEV + offset, 0)
    last = jnp.minimum(first + number, NB)
    return (first.astype(jnp.int32), (last - first).astype(jnp.int32))


def draw_start_block(key, part):
    return window_pair(key)[0]


def draw_block_count(key, part):
    return window_pair(key)[1]


def banded(key, rows, width, centers):
    positions = jnp.arange(rows).astype(jnp.int32)[None, :, None]
    distance = (positions - centers[:, None, :] + width // 2) % rows
    inside = (distance < width).astype(jnp.float32)
    values = jax.random.uniform(jax.random.fold_in(key, 77), (NT, rows, PIX), jnp.float32, 0.5, 1.5)
    return (inside * values / width).astype(jnp.bfloat16)


def draw_column_profile(key, part):
    detector = jnp.arange(PIX).astype(jnp.int32)[None, :]
    tiles = jnp.arange(NT).astype(jnp.int32)[:, None]
    centers = (detector * SX // PIX + tiles * (SX // 7)) % SX
    return banded(jax.random.fold_in(key, 11), SX, max(SX // 32, 4), centers)


def draw_row_profile(key, part):
    detector = jnp.arange(PIX).astype(jnp.int32)[None, :]
    tiles = jnp.arange(NT).astype(jnp.int32)[:, None]
    centers = (detector * 37 + tiles * (SY // 3)) % SY
    return banded(jax.random.fold_in(key, 13), SY, max(SY // 8, 4), centers)


def draw_materials(key, part):
    key_level, key_factor = jax.random.split(jax.random.fold_in(key, 909))
    levels = jax.random.uniform(key_level, (M, NB, 8, 16), jnp.float32, 0.05, 1.0)
    factor = jax.random.uniform(key_factor, (M, NB, SY, SX), jnp.float32, 0.5, 1.0)
    blocky = jnp.repeat(jnp.repeat(levels, SY // 8, axis=2), SX // 16, axis=3)
    return blocky * factor


def with_ends(values, own_key, least, largest):
    longest = values.shape.index(max(values.shape))
    spots = []
    for shift in (0, 1):
        where = [jax.random.randint(jax.random.fold_in(own_key, axis), (), 0, length) for axis, length in enumerate(values.shape)]
        where[longest] = (where[longest] + shift) % values.shape[longest]
        spots.append(tuple(where))
    return values.at[spots[0]].set(least).at[spots[1]].set(largest)


def setup_inputs(seed: int = 0, part: int = 0) -> dict:
    key_of = jax.random.split(jax.random.key(seed), 11)
    part_splits = jax.random.split(jax.random.fold_in(key_of[10], part), 11)
    return {
        "materials": draw_materials(jax.random.fold_in(jax.random.fold_in(key_of[10], part), 71), part),
        "column_profile": draw_column_profile(jax.random.fold_in(key_of[10], 71), part),
        "row_profile": draw_row_profile(jax.random.fold_in(key_of[10], 71), part),
        "start_block": draw_start_block(jax.random.fold_in(jax.random.fold_in(key_of[10], part), 71), part),
        "block_count": draw_block_count(jax.random.fold_in(jax.random.fold_in(key_of[10], part), 71), part),
        "tile_ids": with_ends(jax.random.randint(part_splits[5], (VIEWS, WMAX), 0, NT), jax.random.fold_in(part_splits[5], 1), 0, NT - 1).astype(jnp.int32),
        "photon_counts": with_ends(jax.random.randint(part_splits[6], (VIEWS, E, DROWS, PIX), 0, 3200), jax.random.fold_in(part_splits[6], 1), 0, 3199).astype(jnp.int32),
        "spectrum": jnp.clip(jnp.exp(jax.random.uniform(key_of[7], (E, K), jnp.float32, math.log(20.0), math.log(200.0))), 20.0, 200.0),
        "attenuation": jnp.clip(jnp.exp(jax.random.uniform(key_of[8], (K, M), jnp.float32, math.log(0.05), math.log(0.5))), 0.05, 0.5),
        "step_size": jnp.clip(jnp.exp(jax.random.uniform(key_of[9], (M,), jnp.float32, math.log(0.002), math.log(0.01))), 0.002, 0.01),
    }


def poisson_gradient(line, counts, rowmask, spectrum, attenuation):
    highest = lax.Precision.HIGHEST
    atten_sum = jnp.einsum("km,vmrp->vkrp", attenuation, line, precision=highest)
    trans = jnp.exp(-atten_sum)
    expected = jnp.einsum("ek,vkrp->verp", spectrum, trans, precision=highest)
    weight = 1.0 - counts.astype(jnp.float32) / expected
    back_terms = jnp.einsum("ek,verp->vkrp", spectrum, weight, precision=highest)
    grad_full = -jnp.einsum("km,vkrp->vmrp", attenuation, trans * back_terms, precision=highest)
    return (grad_full * rowmask[:, None, :, None]).astype(jnp.bfloat16)


def reference(materials, column_profile, row_profile, start_block, block_count, tile_ids, photon_counts, spectrum, attenuation, step_size):
    row_slot = jnp.arange(DROWS).astype(jnp.int32)
    for iteration in range(ITERS):
        rounded = materials.astype(jnp.bfloat16)

        def view_step(summed, inputs):
            first, number, tiles_here, counts = inputs
            pieces = []
            for slot_index in range(WMAX):
                block_index = jnp.clip(first + slot_index, 0, NB - 1).astype(jnp.int32)
                valid = (slot_index < number).astype(jnp.float32)
                block_data = lax.dynamic_index_in_dim(rounded, block_index, 1, keepdims=False)
                col_tile = lax.dynamic_index_in_dim(column_profile, tiles_here[slot_index], 0, keepdims=False)
                row_tile = lax.dynamic_index_in_dim(row_profile, tiles_here[slot_index], 0, keepdims=False)
                across = jnp.dot(block_data.reshape(M * SY, SX), col_tile, preferred_element_type=jnp.float32).reshape(M, SY, PIX)
                piece = jnp.sum(across * row_tile.astype(jnp.float32)[None], axis=1)
                pieces.append(piece * valid)
            line = jnp.stack(pieces, axis=1)
            rowmask = (row_slot < number).astype(jnp.float32)
            gradient = poisson_gradient(line[None], counts[None], rowmask[None], spectrum, attenuation)[0]
            for slot_index in range(WMAX):
                block_index = jnp.clip(first + slot_index, 0, NB - 1).astype(jnp.int32)
                valid = (slot_index < number).astype(jnp.float32)
                col_tile = lax.dynamic_index_in_dim(column_profile, tiles_here[slot_index], 0, keepdims=False)
                row_tile = lax.dynamic_index_in_dim(row_profile, tiles_here[slot_index], 0, keepdims=False)
                grad_rows = gradient[:, slot_index, :].astype(jnp.float32)
                weighted = (grad_rows[:, None, :] * row_tile.astype(jnp.float32)[None]).astype(jnp.bfloat16)
                contrib = lax.dot_general(weighted.reshape(M * SY, PIX), col_tile, (((1,), (1,)), ((), ())), preferred_element_type=jnp.float32)
                current = lax.dynamic_index_in_dim(summed, block_index, 1, keepdims=False)
                summed = lax.dynamic_update_index_in_dim(summed, current + valid * contrib.reshape(M, SY, SX), block_index, 1)
            return summed, None

        zeros = jnp.zeros(materials.shape, jnp.float32)
        backprojected, unused = lax.scan(view_step, zeros, (start_block, block_count, tile_ids, photon_counts))
        materials = materials - step_size[:, None, None, None] * backprojected
    return materials
```

```python
import functools

import jax
import jax.numpy as jnp
from jax import lax
from jax.experimental import pallas as pl
from jax.experimental.pallas import tpu as pltpu
from jax.sharding import PartitionSpec as P

ITERS = 2
MESH = pl.DeviceIdType.MESH
F32 = jnp.float32
BF16 = jnp.bfloat16
STEP = 256
REACH = 3
ROWS = 8
TRANSPOSED = (((1,), (1,)), ((), ()))


def project(maps, column, row, lines, cols, s):
    mats, height, width = maps.shape[1:]
    tiles = column.shape[0]
    block = maps[s].reshape(mats * height, width)
    for t in range(tiles):
        across = jnp.dot(block, column[t, :, cols], preferred_element_type=F32)
        across = across.reshape(mats, height, cols.size) * row[t, :, cols].astype(F32)[None]
        lines[s * tiles + t, :, cols] = jnp.sum(across, axis=1)


def first_kernel(
    n,
    start_ref,
    count_ref,
    tiles_ref,
    mats_ref,
    col_ref,
    row_ref,
    counts_ref,
    lines,
    seen,
    maps,
    column,
    row,
    rounded,
    counts,
    send,
    load_sem,
    chunk_sem,
    counts_sem,
    send_sem,
    recv_sem,
):
    me = lax.axis_index("view")
    mats, own, height, width = mats_ref.shape
    tiles, _, columns = col_ref.shape
    bins, window = counts_ref.shape[1:3]
    has_low, has_high = me > 0, me < n - 1
    low, high = jnp.maximum(me - 1, 0), jnp.minimum(me + 1, n - 1)

    def maps_load(s):
        return pltpu.make_async_copy(mats_ref.at[:, s], maps.at[s], load_sem.at[s])

    def chunk_load(which, i):
        cols = pl.ds(i * STEP, STEP)
        source, target = ((col_ref, column), (row_ref, row))[which]
        return pltpu.make_async_copy(source.at[:, :, cols], target.at[:, :, cols], chunk_sem.at[which, i])

    counts_load = pltpu.make_async_copy(counts_ref.at[0], counts, counts_sem)
    counts_load.start()
    maps_load(0).start()
    chunk_load(0, 0).start()
    chunk_load(1, 0).start()
    for s in range(1, own):
        maps_load(s).start()
    for i in range(1, columns // STEP):
        chunk_load(0, i).start()
        chunk_load(1, i).start()

    barrier = pltpu.get_barrier_semaphore()

    @pl.when(has_low)
    def _():
        pl.semaphore_signal(barrier, inc=1, device_id={"view": low}, device_id_type=MESH)

    @pl.when(has_high)
    def _():
        pl.semaphore_signal(barrier, inc=1, device_id={"view": high}, device_id_type=MESH)

    nothing = jnp.concatenate([jnp.zeros((bins, own, columns), F32), jnp.full((1, own, columns), -1.0, F32)], axis=0)

    @pl.when(jnp.logical_not(has_low))
    def _():
        seen[0] = nothing

    @pl.when(jnp.logical_not(has_high))
    def _():
        seen[2] = nothing

    def seen_copy(way):
        return pltpu.make_async_remote_copy(
            src_ref=send.at[way],
            dst_ref=seen.at[0 if way == 0 else 2],
            send_sem=send_sem.at[way],
            recv_sem=recv_sem.at[way],
            device_id={"view": high if way == 0 else low},
            device_id_type=MESH,
        )

    sends = ((0, has_high), (1, has_low))
    receives = ((0, has_low), (1, has_high))

    counts_load.wait()
    start, number = start_ref[0], count_ref[0]
    for target, shift in ((send.at[0], own), (send.at[1], -own), (seen.at[1], 0)):
        for s in range(own):
            j = me * own + shift + s - start
            held = (j >= 0) & (j < number)
            j = jnp.clip(j, 0, window - 1)
            for e in range(bins):
                target[e, s : s + 1] = counts[e, pl.ds(j, 1)].astype(F32)
            code = jnp.where(held, tiles_ref[0, j], -1).astype(F32)
            target[bins, s : s + 1] = jnp.full((1, columns), code, F32)
    pl.semaphore_wait(barrier, has_low.astype(jnp.int32) + has_high.astype(jnp.int32))
    for way, there in sends:

        @pl.when(there)
        def _(way=way):
            seen_copy(way).start()

    for i in range(columns // STEP):
        cols = pl.ds(i * STEP, STEP)
        for s in range(own):
            if i == 0:
                maps_load(s).wait()
                rounded[s] = maps[s].astype(BF16)
            if s == 0:
                chunk_load(0, i).wait()
                chunk_load(1, i).wait()
            project(rounded, column, row, lines, cols, s)

    for way, there in receives:

        @pl.when(there)
        def _(way=way):
            seen_copy(way).wait_recv()

    for way, there in sends:

        @pl.when(there)
        def _(way=way):
            seen_copy(way).wait_send()


def second_kernel(
    spec_ref,
    atten_ref,
    step_ref,
    lines_ref,
    seen_ref,
    maps_ref,
    column,
    row,
    out_ref,
    lines_new,
    counts,
    grad,
    total,
    maps_new,
    rounded,
    result,
    store_sem,
):
    own, mats, height, width = maps_ref.shape
    tiles, _, columns = column.shape
    bins, energies = spec_ref.shape
    last = columns // STEP - 1

    def held_by(cols):
        code = counts[bins, :, cols]
        slot = lax.broadcasted_iota(jnp.int32, code.shape, 0) % own
        return [(code == t) & (slot == s) for s in range(own) for t in range(tiles)]

    def gather(i):
        cols = pl.ds(i * STEP, STEP)
        empty = jnp.zeros((ROWS - REACH * own, STEP), F32)
        for e in range(bins + 1):
            fill = empty if e < bins else empty - 1.0
            counts[e, :, cols] = jnp.concatenate([seen_ref[w, e, :, cols] for w in range(REACH)] + [fill], axis=0)

    def poisson(lines, i):
        cols = pl.ds(i * STEP, STEP)
        held = held_by(cols)
        xs = []
        for m in range(mats):
            x = jnp.zeros((ROWS, STEP), F32)
            for p in range(own * tiles):
                x = jnp.where(held[p], lines[p, m : m + 1, cols], x)
            xs.append(x)
        trans = []
        for k in range(energies):
            exponent = atten_ref[0, k] * xs[0]
            for m in range(1, mats):
                exponent = exponent + atten_ref[m, k] * xs[m]
            trans.append(jnp.exp(-exponent))
        back = [None] * energies
        for e in range(bins):
            expected = spec_ref[e, 0] * trans[0]
            for k in range(1, energies):
                expected = expected + spec_ref[e, k] * trans[k]
            weight = 1.0 - counts[e, :, cols] / expected
            for k in range(energies):
                term = spec_ref[e, k] * weight
                back[k] = term if e == 0 else back[k] + term
        for m in range(mats):
            slope = None
            for k in range(energies):
                term = atten_ref[m, k] * (trans[k] * back[k])
                slope = term if k == 0 else slope + term
            slope = (-slope).astype(BF16).astype(F32)
            for p in range(own * tiles):
                grad[p, m : m + 1, cols] = jnp.sum(jnp.where(held[p], slope, 0.0), axis=0, keepdims=True)

    def back_project(s, cols):
        sums = None
        for t in range(tiles):
            g = grad[s * tiles + t, :, cols]
            profile = row[t, :, cols].astype(F32)
            weighted = jnp.concatenate([(g[m : m + 1] * profile).astype(BF16) for m in range(mats)], axis=0)
            part = lax.dot_general(weighted, column[t, :, cols], TRANSPOSED, preferred_element_type=F32)
            sums = part if t == 0 else sums + part
        return sums

    gather(0)
    poisson(lines_ref, 0)
    for i in range(last + 1):
        cols = pl.ds(i * STEP, STEP)
        if i < last:
            gather(i + 1)
            poisson(lines_ref, i + 1)
        for s in range(own):
            sums = back_project(s, cols)
            if i > 0:
                sums = total[s] + sums
            if i < last:
                total[s] = sums
            else:
                for m in range(mats):
                    new = maps_ref[s, m] - step_ref[m] * sums[m * height : (m + 1) * height]
                    maps_new[s, m] = new
                    rounded[s, m] = new.astype(BF16)
    for i in range(last + 1):
        for s in range(own):
            project(rounded, column, row, lines_new, pl.ds(i * STEP, STEP), s)
        if i > 0:
            poisson(lines_new, i - 1)
    poisson(lines_new, last)
    stores = [
        [pltpu.make_async_copy(result.at[s, m], out_ref.at[m, s], store_sem.at[s, m]) for m in range(mats)]
        for s in range(own)
    ]
    for s in range(own):
        sums = back_project(s, pl.ds(0, last * STEP)) + back_project(s, pl.ds(last * STEP, STEP))
        for m in range(mats):
            result[s, m] = maps_new[s, m] - step_ref[m] * sums[m * height : (m + 1) * height]
            stores[s][m].start()
    for group in stores:
        for copy in group:
            copy.wait()


def solution(mesh):
    n = mesh.shape["view"]

    def local(materials, column_profile, row_profile, start, count, tile_ids, counts, spectrum, attenuation, step):
        mats, own, height, width = materials.shape
        tiles, _, columns = column_profile.shape
        views, bins, window, _ = counts.shape
        assert views == 1 and REACH * own <= ROWS and columns % STEP == 0 and ITERS == 2
        pairs = own * tiles
        vmem = pl.BlockSpec(memory_space=pltpu.VMEM)
        smem = pl.BlockSpec(memory_space=pltpu.SMEM)
        hbm = pl.BlockSpec(memory_space=pltpu.HBM)
        chunks = columns // STEP
        passed = pl.pallas_call(
            functools.partial(first_kernel, n),
            out_shape=[
                pltpu.VMEM((pairs, mats, columns), F32),
                pltpu.VMEM((REACH, bins + 1, own, columns), F32),
                pltpu.VMEM((own, mats, height, width), F32),
                pltpu.VMEM(column_profile.shape, BF16),
                pltpu.VMEM(row_profile.shape, BF16),
            ],
            in_specs=[smem] * 3 + [hbm] * 4,
            out_specs=[vmem] * 5,
            scratch_shapes=[
                pltpu.VMEM((own, mats, height, width), BF16),
                pltpu.VMEM((bins, window, columns), jnp.int32),
                pltpu.VMEM((2, bins + 1, own, columns), F32),
                pltpu.SemaphoreType.DMA((own,)),
                pltpu.SemaphoreType.DMA((2, chunks)),
                pltpu.SemaphoreType.DMA,
                pltpu.SemaphoreType.DMA((2,)),
                pltpu.SemaphoreType.DMA((2,)),
            ],
            compiler_params=pltpu.CompilerParams(
                collective_id=0, has_side_effects=True, vmem_limit_bytes=24 * 1024 * 1024
            ),
        )(
            start,
            count,
            *[
                pltpu.with_memory_space_constraint(x, pltpu.HBM)
                for x in (tile_ids, materials, column_profile, row_profile, counts)
            ],
        )
        return pl.pallas_call(
            second_kernel,
            out_shape=jax.ShapeDtypeStruct(materials.shape, F32),
            in_specs=[smem] * 3 + [vmem] * 5,
            out_specs=hbm,
            scratch_shapes=[
                pltpu.VMEM((pairs, mats, columns), F32),
                pltpu.VMEM((bins + 1, ROWS, columns), F32),
                pltpu.VMEM((pairs, mats, columns), F32),
                pltpu.VMEM((own, mats * height, width), F32),
                pltpu.VMEM((own, mats, height, width), F32),
                pltpu.VMEM((own, mats, height, width), BF16),
                pltpu.VMEM((own, mats, height, width), F32),
                pltpu.SemaphoreType.DMA((own, mats)),
            ],
            compiler_params=pltpu.CompilerParams(vmem_limit_bytes=40 * 1024 * 1024),
        )(spectrum, attenuation.T, step, *passed)

    placed = (
        P(None, ("groups", "view"), None, None),
        P(),
        P(),
        P(("groups", "view")),
        P(("groups", "view")),
        P(("groups", "view"), None),
        P(("groups", "view"), None, None, None),
        P(),
        P(),
        P(),
    )
    return jax.shard_map(
        local,
        mesh=mesh,
        in_specs=placed,
        out_specs=P(None, ("groups", "view"), None, None),
        check_vma=False,
    )
```

```python
import functools

import jax
import jax.numpy as jnp
from jax import lax
from jax.experimental import pallas as pl
from jax.experimental.pallas import tpu as pltpu
from jax.sharding import PartitionSpec as P

ITERS = 2
MESH = pl.DeviceIdType.MESH
F32 = jnp.float32
BF16 = jnp.bfloat16
STEP = 256
REACH = 3
ROWS = 8
TRANSPOSED = (((1,), (1,)), ((), ()))


def project(maps, column, row, lines, cols, s):
    mats, height, width = maps.shape[1:]
    tiles = column.shape[0]
    block = maps[s].reshape(mats * height, width)
    for t in range(tiles):
        across = jnp.dot(block, column[t, :, cols], preferred_element_type=F32)
        across = across.reshape(mats, height, cols.size) * row[t, :, cols].astype(F32)[None]
        lines[s * tiles + t, :, cols] = jnp.sum(across, axis=1)


def first_kernel(
    n,
    start_hbm,
    count_hbm,
    tiles_hbm,
    mats_ref,
    col_ref,
    row_ref,
    counts_ref,
    lines,
    seen,
    maps,
    column,
    row,
    rounded,
    counts,
    send,
    start_ref,
    count_ref,
    tiles_ref,
    load_sem,
    chunk_sem,
    counts_sem,
    small_sem,
    send_sem,
    recv_sem,
):
    me = lax.axis_index("view")
    mats, own, height, width = mats_ref.shape
    tiles, _, columns = col_ref.shape
    bins, window = counts_ref.shape[1:3]
    has_low, has_high = me > 0, me < n - 1
    low, high = jnp.maximum(me - 1, 0), jnp.minimum(me + 1, n - 1)

    def maps_load(s):
        return pltpu.make_async_copy(mats_ref.at[:, s], maps.at[s], load_sem.at[s])

    def chunk_load(which, i):
        cols = pl.ds(i * STEP, STEP)
        source, target = ((col_ref, column), (row_ref, row))[which]
        return pltpu.make_async_copy(source.at[:, :, cols], target.at[:, :, cols], chunk_sem.at[which, i])

    counts_load = pltpu.make_async_copy(counts_ref.at[0], counts, counts_sem)
    smalls = [
        pltpu.make_async_copy(source, target, small_sem.at[i])
        for i, (source, target) in enumerate(((start_hbm, start_ref), (count_hbm, count_ref), (tiles_hbm, tiles_ref)))
    ]
    for copy in smalls:
        copy.start()
    counts_load.start()
    maps_load(0).start()
    chunk_load(0, 0).start()
    chunk_load(1, 0).start()
    for i in range(1, columns // STEP):
        chunk_load(0, i).start(priority=1)
        chunk_load(1, i).start(priority=1)
    for r in range(1, own):
        maps_load(r).start(priority=1)
    barrier = pltpu.get_barrier_semaphore()

    @pl.when(has_low)
    def _():
        pl.semaphore_signal(barrier, inc=1, device_id={"view": low}, device_id_type=MESH)

    @pl.when(has_high)
    def _():
        pl.semaphore_signal(barrier, inc=1, device_id={"view": high}, device_id_type=MESH)

    nothing = jnp.concatenate([jnp.zeros((bins, own, columns), F32), jnp.full((1, own, columns), -1.0, F32)], axis=0)

    @pl.when(jnp.logical_not(has_low))
    def _():
        seen[0] = nothing

    @pl.when(jnp.logical_not(has_high))
    def _():
        seen[2] = nothing

    def seen_copy(way):
        return pltpu.make_async_remote_copy(
            src_ref=send.at[way],
            dst_ref=seen.at[0 if way == 0 else 2],
            send_sem=send_sem.at[way],
            recv_sem=recv_sem.at[way],
            device_id={"view": high if way == 0 else low},
            device_id_type=MESH,
        )

    sends = ((0, has_high), (1, has_low))
    receives = ((0, has_low), (1, has_high))

    def exchange():
        for copy in smalls:
            copy.wait()
        counts_load.wait()
        start, number = start_ref[0, 0], count_ref[0, 0]
        for target, shift in ((send.at[0], own), (send.at[1], -own), (seen.at[1], 0)):
            for s in range(own):
                j = me * own + shift + s - start
                held = (j >= 0) & (j < number)
                j = jnp.clip(j, 0, window - 1)
                for e in range(bins):
                    target[e, s : s + 1] = counts[e, pl.ds(j, 1)].astype(F32)
                code = jnp.where(held, tiles_ref[0, j], -1).astype(F32)
                target[bins, s : s + 1] = jnp.full((1, columns), code, F32)
        pl.semaphore_wait(barrier, has_low.astype(jnp.int32) + has_high.astype(jnp.int32))
        for way, there in sends:

            @pl.when(there)
            def _(way=way):
                seen_copy(way).start()


    for s in range(own):
        maps_load(s).wait()
        rounded[s] = maps[s].astype(BF16)
        for i in range(columns // STEP):
            if s == 0:
                chunk_load(0, i).wait()
                chunk_load(1, i).wait()
            project(rounded, column, row, lines, pl.ds(i * STEP, STEP), s)
            if s == 0 and i == 0:
                exchange()

    for way, there in receives:

        @pl.when(there)
        def _(way=way):
            seen_copy(way).wait_recv()

    for way, there in sends:

        @pl.when(there)
        def _(way=way):
            seen_copy(way).wait_send()


def second_kernel(
    spec_ref,
    atten_ref,
    step_ref,
    lines_ref,
    seen_ref,
    maps_ref,
    column,
    row,
    out_ref,
    lines_new,
    counts,
    grad,
    total,
    maps_new,
    rounded,
    result,
    store_sem,
):
    own, mats, height, width = maps_ref.shape
    tiles, _, columns = column.shape
    bins, energies = spec_ref.shape
    last = columns // STEP - 1

    def held_by(cols):
        code = counts[bins, :, cols]
        slot = lax.broadcasted_iota(jnp.int32, code.shape, 0) % own
        return [(code == t) & (slot == s) for s in range(own) for t in range(tiles)]

    def gather(i):
        cols = pl.ds(i * STEP, STEP)
        empty = jnp.zeros((ROWS - REACH * own, STEP), F32)
        for e in range(bins + 1):
            fill = empty if e < bins else empty - 1.0
            counts[e, :, cols] = jnp.concatenate([seen_ref[w, e, :, cols] for w in range(REACH)] + [fill], axis=0)

    def poisson(lines, i):
        cols = pl.ds(i * STEP, STEP)
        held = held_by(cols)
        xs = []
        for m in range(mats):
            x = jnp.zeros((ROWS, STEP), F32)
            for p in range(own * tiles):
                x = jnp.where(held[p], lines[p, m : m + 1, cols], x)
            xs.append(x)
        trans = []
        for k in range(energies):
            exponent = atten_ref[0, k] * xs[0]
            for m in range(1, mats):
                exponent = exponent + atten_ref[m, k] * xs[m]
            trans.append(jnp.exp(-exponent))
        back = [None] * energies
        for e in range(bins):
            expected = spec_ref[e, 0] * trans[0]
            for k in range(1, energies):
                expected = expected + spec_ref[e, k] * trans[k]
            weight = 1.0 - counts[e, :, cols] / expected
            for k in range(energies):
                term = spec_ref[e, k] * weight
                back[k] = term if e == 0 else back[k] + term
        for m in range(mats):
            slope = None
            for k in range(energies):
                term = atten_ref[m, k] * (trans[k] * back[k])
                slope = term if k == 0 else slope + term
            slope = (-slope).astype(BF16).astype(F32)
            for p in range(own * tiles):
                grad[p, m : m + 1, cols] = jnp.sum(jnp.where(held[p], slope, 0.0), axis=0, keepdims=True)

    def back_project(s, cols):
        sums = None
        for t in range(tiles):
            g = grad[s * tiles + t, :, cols]
            profile = row[t, :, cols].astype(F32)
            weighted = jnp.concatenate([(g[m : m + 1] * profile).astype(BF16) for m in range(mats)], axis=0)
            part = lax.dot_general(weighted, column[t, :, cols], TRANSPOSED, preferred_element_type=F32)
            sums = part if t == 0 else sums + part
        return sums

    gather(0)
    poisson(lines_ref, 0)
    for i in range(last + 1):
        cols = pl.ds(i * STEP, STEP)
        if i < last:
            gather(i + 1)
            poisson(lines_ref, i + 1)
        for s in range(own):
            sums = back_project(s, cols)
            if i > 0:
                sums = total[s] + sums
            if i < last:
                total[s] = sums
            else:
                for m in range(mats):
                    new = maps_ref[s, m] - step_ref[m] * sums[m * height : (m + 1) * height]
                    maps_new[s, m] = new
                    rounded[s, m] = new.astype(BF16)
    for i in range(last + 1):
        for s in range(own):
            project(rounded, column, row, lines_new, pl.ds(i * STEP, STEP), s)
        if i > 0:
            poisson(lines_new, i - 1)
    poisson(lines_new, last)
    stores = [
        [pltpu.make_async_copy(result.at[s, m], out_ref.at[m, s], store_sem.at[s, m]) for m in range(mats)]
        for s in range(own)
    ]
    for s in range(own):
        sums = back_project(s, pl.ds(0, last * STEP)) + back_project(s, pl.ds(last * STEP, STEP))
        for m in range(mats):
            result[s, m] = maps_new[s, m] - step_ref[m] * sums[m * height : (m + 1) * height]
            stores[s][m].start()
    for group in stores:
        for copy in group:
            copy.wait()


def solution(mesh):
    n = mesh.shape["view"]

    def local(materials, column_profile, row_profile, start, count, tile_ids, counts, spectrum, attenuation, step):
        mats, own, height, width = materials.shape
        tiles, _, columns = column_profile.shape
        views, bins, window, _ = counts.shape
        assert views == 1 and REACH * own <= ROWS and columns % STEP == 0 and ITERS == 2
        pairs = own * tiles
        vmem = pl.BlockSpec(memory_space=pltpu.VMEM)
        smem = pl.BlockSpec(memory_space=pltpu.SMEM)
        hbm = pl.BlockSpec(memory_space=pltpu.HBM)
        chunks = columns // STEP
        passed = pl.pallas_call(
            functools.partial(first_kernel, n),
            out_shape=[
                pltpu.VMEM((pairs, mats, columns), F32),
                pltpu.VMEM((REACH, bins + 1, own, columns), F32),
                pltpu.VMEM((own, mats, height, width), F32),
                pltpu.VMEM(column_profile.shape, BF16),
                pltpu.VMEM(row_profile.shape, BF16),
            ],
            in_specs=[hbm] * 7,
            out_specs=[vmem] * 5,
            scratch_shapes=[
                pltpu.VMEM((own, mats, height, width), BF16),
                pltpu.VMEM((bins, window, columns), jnp.int32),
                pltpu.VMEM((2, bins + 1, own, columns), F32),
                pltpu.SMEM((1, 1), jnp.int32),
                pltpu.SMEM((1, 1), jnp.int32),
                pltpu.SMEM(tile_ids.shape, jnp.int32),
                pltpu.SemaphoreType.DMA((own,)),
                pltpu.SemaphoreType.DMA((2, chunks)),
                pltpu.SemaphoreType.DMA,
                pltpu.SemaphoreType.DMA((3,)),
                pltpu.SemaphoreType.DMA((2,)),
                pltpu.SemaphoreType.DMA((2,)),
            ],
            compiler_params=pltpu.CompilerParams(
                collective_id=0, has_side_effects=True, vmem_limit_bytes=24 * 1024 * 1024
            ),
        )(
            start.reshape(1, 1),
            count.reshape(1, 1),
            *[
                pltpu.with_memory_space_constraint(x, pltpu.HBM)
                for x in (tile_ids, materials, column_profile, row_profile, counts)
            ],
        )
        return pl.pallas_call(
            second_kernel,
            out_shape=jax.ShapeDtypeStruct(materials.shape, F32),
            in_specs=[smem] * 3 + [vmem] * 5,
            out_specs=hbm,
            scratch_shapes=[
                pltpu.VMEM((pairs, mats, columns), F32),
                pltpu.VMEM((bins + 1, ROWS, columns), F32),
                pltpu.VMEM((pairs, mats, columns), F32),
                pltpu.VMEM((own, mats * height, width), F32),
                pltpu.VMEM((own, mats, height, width), F32),
                pltpu.VMEM((own, mats, height, width), BF16),
                pltpu.VMEM((own, mats, height, width), F32),
                pltpu.SemaphoreType.DMA((own, mats)),
            ],
            compiler_params=pltpu.CompilerParams(vmem_limit_bytes=40 * 1024 * 1024),
        )(spectrum, attenuation.T, step, *passed)

    placed = (
        P(None, ("groups", "view"), None, None),
        P(),
        P(),
        P(("groups", "view")),
        P(("groups", "view")),
        P(("groups", "view"), None),
        P(("groups", "view"), None, None, None),
        P(),
        P(),
        P(),
    )
    return jax.shard_map(
        local,
        mesh=mesh,
        in_specs=placed,
        out_specs=P(None, ("groups", "view"), None, None),
        check_vma=False,
    )
```

```python
import functools

import jax
import jax.numpy as jnp
from jax import lax
from jax.experimental import pallas as pl
from jax.experimental.pallas import tpu as pltpu
from jax.sharding import PartitionSpec as P

ITERS = 2
MESH = pl.DeviceIdType.MESH
F32 = jnp.float32
BF16 = jnp.bfloat16
STEP = 256
LANES = 128
REACH = 3
ROWS = 8
TRANSPOSED = (((1,), (1,)), ((), ()))


def project(block, column, row, lines, cols, to, s):
    mats, height, width = block.shape
    tiles = column.shape[0]
    for t in range(tiles):
        across = jnp.dot(block[...].reshape(mats * height, width), column[t, :, cols], preferred_element_type=F32)
        across = across.reshape(mats, height, cols.size) * row[t, :, cols].astype(F32)[None]
        lines[s * tiles + t, :, to] = jnp.sum(across, axis=1)


def first_kernel(
    n,
    start_hbm,
    count_hbm,
    tiles_hbm,
    mats_ref,
    col_ref,
    row_ref,
    counts_ref,
    lines,
    seen,
    maps,
    column,
    row,
    rounded,
    counts,
    send,
    start_ref,
    count_ref,
    tiles_ref,
    load_sem,
    chunk_sem,
    counts_sem,
    small_sem,
    send_sem,
    recv_sem,
):
    me = lax.axis_index("view")
    mats, own, height, width = mats_ref.shape
    tiles, _, columns = col_ref.shape
    bins, window = counts_ref.shape[1:3]
    has_low, has_high = me > 0, me < n - 1
    low, high = jnp.maximum(me - 1, 0), jnp.minimum(me + 1, n - 1)

    def maps_load(s):
        return pltpu.make_async_copy(mats_ref.at[:, s], maps.at[s], load_sem.at[s])

    def chunk_load(which, i):
        cols = pl.ds(i * STEP, STEP)
        source, target = ((col_ref, column), (row_ref, row))[which]
        return pltpu.make_async_copy(source.at[:, :, cols], target.at[:, :, cols], chunk_sem.at[which, i])

    counts_load = pltpu.make_async_copy(counts_ref.at[0], counts, counts_sem)
    smalls = [
        pltpu.make_async_copy(source, target, small_sem.at[i])
        for i, (source, target) in enumerate(((start_hbm, start_ref), (count_hbm, count_ref), (tiles_hbm, tiles_ref)))
    ]
    for copy in smalls:
        copy.start()
    counts_load.start()
    maps_load(0).start()
    chunk_load(0, 0).start()
    chunk_load(1, 0).start()
    for i in range(1, columns // STEP):
        chunk_load(0, i).start(priority=1)
        chunk_load(1, i).start(priority=1)
    for r in range(1, own):
        maps_load(r).start(priority=1)
    barrier = pltpu.get_barrier_semaphore()

    @pl.when(has_low)
    def _():
        pl.semaphore_signal(barrier, inc=1, device_id={"view": low}, device_id_type=MESH)

    @pl.when(has_high)
    def _():
        pl.semaphore_signal(barrier, inc=1, device_id={"view": high}, device_id_type=MESH)

    nothing = jnp.concatenate([jnp.zeros((bins, own, columns), F32), jnp.full((1, own, columns), -1.0, F32)], axis=0)

    @pl.when(jnp.logical_not(has_low))
    def _():
        seen[0] = nothing

    @pl.when(jnp.logical_not(has_high))
    def _():
        seen[2] = nothing

    def seen_copy(way):
        return pltpu.make_async_remote_copy(
            src_ref=send.at[way],
            dst_ref=seen.at[0 if way == 0 else 2],
            send_sem=send_sem.at[way],
            recv_sem=recv_sem.at[way],
            device_id={"view": high if way == 0 else low},
            device_id_type=MESH,
        )

    sends = ((0, has_high), (1, has_low))
    receives = ((0, has_low), (1, has_high))

    def select():
        for copy in smalls:
            copy.wait()
        counts_load.wait()
        start, number = start_ref[0, 0], count_ref[0, 0]
        for target, shift in ((send.at[0], own), (send.at[1], -own), (seen.at[1], 0)):
            for s in range(own):
                j = me * own + shift + s - start
                held = (j >= 0) & (j < number)
                j = jnp.clip(j, 0, window - 1)
                for e in range(bins):
                    target[e, s : s + 1] = counts[e, pl.ds(j, 1)].astype(F32)
                code = jnp.where(held, tiles_ref[0, j], -1).astype(F32)
                target[bins, s : s + 1] = jnp.full((1, columns), code, F32)

    def exchange():
        pl.semaphore_wait(barrier, has_low.astype(jnp.int32) + has_high.astype(jnp.int32))
        for way, there in sends:

            @pl.when(there)
            def _(way=way):
                seen_copy(way).start()


    select()
    pl.when(me % 2 == 0)(exchange)
    for s in range(own):
        maps_load(s).wait()
        rounded[s] = maps[s].astype(BF16)
        for i in range(columns // STEP):
            if s == 0 and i < 2:
                for j in range(1) if i == 0 else range(1, columns // STEP):
                    chunk_load(0, j).wait()
                    chunk_load(1, j).wait()
            project(rounded.at[s], column, row, lines, pl.ds(i * STEP, STEP), pl.ds(i * STEP, STEP), s)
            if s == 0 and i == 0:
                pl.when(me % 2 == 1)(exchange)

    for way, there in receives:

        @pl.when(there)
        def _(way=way):
            seen_copy(way).wait_recv()

    for way, there in sends:

        @pl.when(there)
        def _(way=way):
            seen_copy(way).wait_send()


def second_kernel(
    spec_ref,
    atten_ref,
    step_ref,
    lines_ref,
    seen_ref,
    maps_ref,
    column,
    row,
    out_ref,
    lines_new,
    counts,
    grad,
    total,
    maps_new,
    rounded,
    result,
    table,
    store_sem,
):
    own, mats, height, width = maps_ref.shape
    tiles, _, columns = column.shape
    bins, energies = spec_ref.shape
    last = columns // STEP - 1

    atten_at = bins * energies
    for e in range(bins):
        for k in range(energies):
            table[e * energies + k] = jnp.full((ROWS, LANES), spec_ref[e, k], F32)
    for m in range(mats):
        for k in range(energies):
            table[atten_at + m * energies + k] = jnp.full((ROWS, LANES), atten_ref[m, k], F32)

    def fixed(at):
        return jnp.concatenate([table[at]] * (STEP // LANES), axis=1)

    def held_by(i):
        code = counts[i][bins]
        slot = lax.broadcasted_iota(jnp.int32, code.shape, 0) % own
        return [(code == t) & (slot == s) for s in range(own) for t in range(tiles)]

    def gather(i):
        cols = pl.ds(i * STEP, STEP)
        empty = jnp.zeros((ROWS - REACH * own, STEP), F32)
        for e in range(bins + 1):
            fill = empty if e < bins else empty - 1.0
            counts[i][e] = jnp.concatenate([seen_ref[w, e, :, cols] for w in range(REACH)] + [fill], axis=0)

    def poisson(i, lines, cols):
        held = held_by(i)
        xs = []
        for m in range(mats):
            x = jnp.zeros((ROWS, STEP), F32)
            for p in range(own * tiles):
                x = jnp.where(held[p], lines[p, m : m + 1, cols], x)
            xs.append(x)
        trans = []
        for k in range(energies):
            exponent = fixed(atten_at + k) * xs[0]
            for m in range(1, mats):
                exponent = exponent + fixed(atten_at + m * energies + k) * xs[m]
            trans.append(jnp.exp(-exponent))
        back = [None] * energies
        for e in range(bins):
            expected = fixed(e * energies) * trans[0]
            for k in range(1, energies):
                expected = expected + fixed(e * energies + k) * trans[k]
            weight = 1.0 - counts[i][e] / expected
            for k in range(energies):
                term = fixed(e * energies + k) * weight
                back[k] = term if e == 0 else back[k] + term
        for m in range(mats):
            slope = None
            for k in range(energies):
                term = fixed(atten_at + m * energies + k) * (trans[k] * back[k])
                slope = term if k == 0 else slope + term
            slope = (-slope).astype(BF16).astype(F32)
            for p in range(own * tiles):
                grad[i][p, m : m + 1] = jnp.sum(jnp.where(held[p], slope, 0.0), axis=0, keepdims=True)

    def back_project(s, first, end, group=None):
        sums = None
        for t in range(tiles):
            blocks = []
            for i in range(first, end):
                g = grad[i][s * tiles + t]
                profile = row[t, :, i * STEP : (i + 1) * STEP].astype(F32)
                blocks.append(
                    jnp.concatenate([(g[m : m + 1] * profile).astype(BF16) for m in group or range(mats)], axis=0)
                )
            weighted = jnp.concatenate(blocks, axis=1)
            part = lax.dot_general(
                weighted, column[t, :, first * STEP : end * STEP], TRANSPOSED, preferred_element_type=F32
            )
            sums = part if t == 0 else sums + part
        return sums

    every = pl.ds(0, STEP)
    gather(0)
    poisson(0, lines_ref, every)
    for i in range(last + 1):
        if i < last:
            gather(i + 1)
            poisson(i + 1, lines_ref, pl.ds((i + 1) * STEP, STEP))
        for s in range(own):
            sums = back_project(s, i, i + 1)
            if i > 0:
                sums = total[s][...] + sums
            if i < last:
                total[s][...] = sums
            else:
                for m in range(mats):
                    new = maps_ref[s, m] - step_ref[m] * sums[m * height : (m + 1) * height]
                    maps_new[s][m] = new
                    rounded[s][m] = new.astype(BF16)
    for i in range(last + 1):
        for s in range(own):
            project(rounded[s], column, row, lines_new[i], pl.ds(i * STEP, STEP), every, s)
        if i > 0:
            poisson(i - 1, lines_new[i - 1], every)
    poisson(last, lines_new[last], every)
    stores = []
    for s in range(own):
        groups = [range(mats)] if s < own - 1 else [range(m, m + 1) for m in range(mats)]
        for group in groups:
            sums = back_project(s, 0, last, group) + back_project(s, last, last + 1, group)
            for i, m in enumerate(group):
                result[s][m] = maps_new[s][m] - step_ref[m] * sums[i * height : (i + 1) * height]
                copy = pltpu.make_async_copy(result[s].at[m], out_ref.at[m, s], store_sem.at[s, m])
                copy.start()
                stores.append(copy)
    for copy in stores:
        copy.wait()


def solution(mesh):
    n = mesh.shape["view"]

    def local(materials, column_profile, row_profile, start, count, tile_ids, counts, spectrum, attenuation, step):
        mats, own, height, width = materials.shape
        tiles, _, columns = column_profile.shape
        views, bins, window, _ = counts.shape
        energies = spectrum.shape[1]
        assert views == 1 and REACH * own <= ROWS and columns % STEP == 0 and ITERS == 2
        pairs = own * tiles
        vmem = pl.BlockSpec(memory_space=pltpu.VMEM)
        smem = pl.BlockSpec(memory_space=pltpu.SMEM)
        hbm = pl.BlockSpec(memory_space=pltpu.HBM)
        chunks = columns // STEP
        passed = pl.pallas_call(
            functools.partial(first_kernel, n),
            out_shape=[
                pltpu.VMEM((pairs, mats, columns), F32),
                pltpu.VMEM((REACH, bins + 1, own, columns), F32),
                pltpu.VMEM((own, mats, height, width), F32),
                pltpu.VMEM(column_profile.shape, BF16),
                pltpu.VMEM(row_profile.shape, BF16),
            ],
            in_specs=[hbm] * 7,
            out_specs=[vmem] * 5,
            scratch_shapes=[
                pltpu.VMEM((own, mats, height, width), BF16),
                pltpu.VMEM((bins, window, columns), jnp.int32),
                pltpu.VMEM((2, bins + 1, own, columns), F32),
                pltpu.SMEM((1, 1), jnp.int32),
                pltpu.SMEM((1, 1), jnp.int32),
                pltpu.SMEM(tile_ids.shape, jnp.int32),
                pltpu.SemaphoreType.DMA((own,)),
                pltpu.SemaphoreType.DMA((2, chunks)),
                pltpu.SemaphoreType.DMA,
                pltpu.SemaphoreType.DMA((3,)),
                pltpu.SemaphoreType.DMA((2,)),
                pltpu.SemaphoreType.DMA((2,)),
            ],
            compiler_params=pltpu.CompilerParams(
                collective_id=0, has_side_effects=True, vmem_limit_bytes=24 * 1024 * 1024
            ),
        )(
            start.reshape(1, 1),
            count.reshape(1, 1),
            *[
                pltpu.with_memory_space_constraint(x, pltpu.HBM)
                for x in (tile_ids, materials, column_profile, row_profile, counts)
            ],
        )
        return pl.pallas_call(
            second_kernel,
            out_shape=jax.ShapeDtypeStruct(materials.shape, F32),
            in_specs=[smem] * 3 + [vmem] * 5,
            out_specs=hbm,
            scratch_shapes=[
                [pltpu.VMEM((pairs, mats, STEP), F32)] * chunks,
                [pltpu.VMEM((bins + 1, ROWS, STEP), F32)] * chunks,
                [pltpu.VMEM((pairs, mats, STEP), F32)] * chunks,
                [pltpu.VMEM((mats * height, width), F32)] * own,
                [pltpu.VMEM((mats, height, width), F32)] * own,
                [pltpu.VMEM((mats, height, width), BF16)] * own,
                [pltpu.VMEM((mats, height, width), F32)] * own,
                pltpu.VMEM(((bins + mats) * energies, ROWS, LANES), F32),
                pltpu.SemaphoreType.DMA((own, mats)),
            ],
            compiler_params=pltpu.CompilerParams(vmem_limit_bytes=40 * 1024 * 1024),
        )(spectrum, attenuation.T, step, *passed)

    placed = (
        P(None, ("groups", "view"), None, None),
        P(),
        P(),
        P(("groups", "view")),
        P(("groups", "view")),
        P(("groups", "view"), None),
        P(("groups", "view"), None, None, None),
        P(),
        P(),
        P(),
    )
    return jax.shard_map(
        local,
        mesh=mesh,
        in_specs=placed,
        out_specs=P(None, ("groups", "view"), None, None),
        check_vma=False,
    )
```

```python
import functools

import jax
import jax.numpy as jnp
from jax import lax
from jax.experimental import pallas as pl
from jax.experimental.pallas import tpu as pltpu
from jax.sharding import PartitionSpec as P

ITERS = 2
MESH = pl.DeviceIdType.MESH
F32 = jnp.float32
BF16 = jnp.bfloat16
STEP = 256
LANES = 128
REACH = 3
ROWS = 8
TRANSPOSED = (((1,), (1,)), ((), ()))


def project(block, column, row, lines, cols, to, s):
    mats, height, width = block.shape
    tiles = column.shape[0]
    for t in range(tiles):
        across = jnp.dot(block[...].reshape(mats * height, width), column[t, :, cols], preferred_element_type=F32)
        across = across.reshape(mats, height, cols.size) * row[t, :, cols].astype(F32)[None]
        lines[s * tiles + t, :, to] = jnp.sum(across, axis=1)


def first_kernel(
    n,
    start_hbm,
    count_hbm,
    tiles_hbm,
    mats_ref,
    col_ref,
    row_ref,
    counts_ref,
    lines,
    seen,
    maps,
    column,
    row,
    rounded,
    counts,
    send,
    start_ref,
    count_ref,
    tiles_ref,
    load_sem,
    chunk_sem,
    counts_sem,
    small_sem,
    send_sem,
    recv_sem,
):
    me = lax.axis_index("view")
    mats, own, height, width = mats_ref.shape
    tiles, _, columns = col_ref.shape
    bins, window = counts_ref.shape[1:3]
    has_low, has_high = me > 0, me < n - 1
    low, high = jnp.maximum(me - 1, 0), jnp.minimum(me + 1, n - 1)

    def maps_load(s):
        return pltpu.make_async_copy(mats_ref.at[:, s], maps.at[s], load_sem.at[s])

    def chunk_load(which, i):
        cols = pl.ds(i * STEP, STEP)
        source, target = ((col_ref, column), (row_ref, row))[which]
        return pltpu.make_async_copy(source.at[:, :, cols], target.at[:, :, cols], chunk_sem.at[which, i])

    counts_load = pltpu.make_async_copy(counts_ref.at[0], counts, counts_sem)
    smalls = [
        pltpu.make_async_copy(source, target, small_sem.at[i])
        for i, (source, target) in enumerate(((start_hbm, start_ref), (count_hbm, count_ref), (tiles_hbm, tiles_ref)))
    ]
    for copy in smalls:
        copy.start()
    counts_load.start()
    maps_load(0).start()
    chunk_load(0, 0).start()
    chunk_load(1, 0).start()
    for i in range(1, columns // STEP):
        chunk_load(0, i).start(priority=1)
        chunk_load(1, i).start(priority=1)
    for r in range(1, own):
        maps_load(r).start(priority=1)
    barrier = pltpu.get_barrier_semaphore()

    @pl.when(has_low)
    def _():
        pl.semaphore_signal(barrier, inc=1, device_id={"view": low}, device_id_type=MESH)

    @pl.when(has_high)
    def _():
        pl.semaphore_signal(barrier, inc=1, device_id={"view": high}, device_id_type=MESH)

    nothing = jnp.concatenate([jnp.zeros((bins, own, columns), F32), jnp.full((1, own, columns), -1.0, F32)], axis=0)

    @pl.when(jnp.logical_not(has_low))
    def _():
        seen[0] = nothing

    @pl.when(jnp.logical_not(has_high))
    def _():
        seen[2] = nothing

    def seen_copy(way):
        return pltpu.make_async_remote_copy(
            src_ref=send.at[way],
            dst_ref=seen.at[0 if way == 0 else 2],
            send_sem=send_sem.at[way],
            recv_sem=recv_sem.at[way],
            device_id={"view": high if way == 0 else low},
            device_id_type=MESH,
        )

    sends = ((0, has_high), (1, has_low))
    receives = ((0, has_low), (1, has_high))

    def select():
        for copy in smalls:
            copy.wait()
        counts_load.wait()
        start, number = start_ref[0, 0], count_ref[0, 0]
        for target, shift in ((send.at[0], own), (send.at[1], -own), (seen.at[1], 0)):
            for s in range(own):
                j = me * own + shift + s - start
                held = (j >= 0) & (j < number)
                j = jnp.clip(j, 0, window - 1)
                for e in range(bins):
                    target[e, s : s + 1] = counts[e, pl.ds(j, 1)].astype(F32)
                code = jnp.where(held, tiles_ref[0, j], -1).astype(F32)
                target[bins, s : s + 1] = jnp.full((1, columns), code, F32)

    def exchange():
        pl.semaphore_wait(barrier, has_low.astype(jnp.int32) + has_high.astype(jnp.int32))
        for way, there in sends:

            @pl.when(there)
            def _(way=way):
                seen_copy(way).start()


    select()
    pl.when(me % 2 == 0)(exchange)
    for s in range(own):
        maps_load(s).wait()
        rounded[s] = maps[s].astype(BF16)
        for i in range(columns // STEP):
            if s == 0 and i < 2:
                for j in range(1) if i == 0 else range(1, columns // STEP):
                    chunk_load(0, j).wait()
                    chunk_load(1, j).wait()
            project(rounded.at[s], column, row, lines, pl.ds(i * STEP, STEP), pl.ds(i * STEP, STEP), s)
            if s == 0 and i == 0:
                pl.when(me % 2 == 1)(exchange)

    for way, there in receives:

        @pl.when(there)
        def _(way=way):
            seen_copy(way).wait_recv()

    for way, there in sends:

        @pl.when(there)
        def _(way=way):
            seen_copy(way).wait_send()


def second_kernel(
    spec_ref,
    atten_ref,
    step_ref,
    lines_ref,
    seen_ref,
    maps_ref,
    column,
    row,
    out_ref,
    lines_new,
    counts,
    grad,
    total,
    maps_new,
    rounded,
    result,
    table,
    store_sem,
):
    own, mats, height, width = maps_ref.shape
    tiles, _, columns = column.shape
    bins, energies = spec_ref.shape
    last = columns // STEP - 1

    atten_at = bins * energies
    for e in range(bins):
        for k in range(energies):
            table[e * energies + k] = jnp.full((ROWS, LANES), spec_ref[e, k], F32)
    for m in range(mats):
        for k in range(energies):
            table[atten_at + m * energies + k] = jnp.full((ROWS, LANES), atten_ref[m, k], F32)

    def fixed(at):
        return jnp.concatenate([table[at]] * (STEP // LANES), axis=1)

    def held_by(i):
        code = counts[i][bins]
        slot = lax.broadcasted_iota(jnp.int32, code.shape, 0) % own
        return [(code == t) & (slot == s) for s in range(own) for t in range(tiles)]

    def gather(i):
        cols = pl.ds(i * STEP, STEP)
        empty = jnp.zeros((ROWS - REACH * own, STEP), F32)
        for e in range(bins + 1):
            fill = empty if e < bins else empty - 1.0
            counts[i][e] = jnp.concatenate([seen_ref[w, e, :, cols] for w in range(REACH)] + [fill], axis=0)

    def poisson(i, lines, cols):
        held = held_by(i)
        xs = []
        for m in range(mats):
            x = jnp.zeros((ROWS, STEP), F32)
            for p in range(own * tiles):
                x = jnp.where(held[p], lines[p, m : m + 1, cols], x)
            xs.append(x)
        trans = []
        for k in range(energies):
            exponent = fixed(atten_at + k) * xs[0]
            for m in range(1, mats):
                exponent = exponent + fixed(atten_at + m * energies + k) * xs[m]
            trans.append(jnp.exp(-exponent))
        back = [None] * energies
        for e in range(bins):
            expected = fixed(e * energies) * trans[0]
            for k in range(1, energies):
                expected = expected + fixed(e * energies + k) * trans[k]
            weight = 1.0 - counts[i][e] / expected
            for k in range(energies):
                term = fixed(e * energies + k) * weight
                back[k] = term if e == 0 else back[k] + term
        for m in range(mats):
            slope = None
            for k in range(energies):
                term = fixed(atten_at + m * energies + k) * (trans[k] * back[k])
                slope = term if k == 0 else slope + term
            slope = (-slope).astype(BF16).astype(F32)
            for p in range(own * tiles):
                grad[i][p, m : m + 1] = jnp.sum(jnp.where(held[p], slope, 0.0), axis=0, keepdims=True)

    def back_project(s, first, end, group=None):
        sums = None
        for t in range(tiles):
            blocks = []
            for i in range(first, end):
                g = grad[i][s * tiles + t]
                profile = row[t, :, i * STEP : (i + 1) * STEP].astype(F32)
                blocks.append(
                    jnp.concatenate([(g[m : m + 1] * profile).astype(BF16) for m in group or range(mats)], axis=0)
                )
            weighted = jnp.concatenate(blocks, axis=1)
            part = lax.dot_general(
                weighted, column[t, :, first * STEP : end * STEP], TRANSPOSED, preferred_element_type=F32
            )
            sums = part if t == 0 else sums + part
        return sums

    every = pl.ds(0, STEP)
    gather(0)
    poisson(0, lines_ref, every)
    for first, end in ((0, 1), (1, last + 1)):
        if first == 0:
            for i in range(end, last + 1):
                gather(i)
                poisson(i, lines_ref, pl.ds(i * STEP, STEP))
        for s in range(own):
            sums = back_project(s, first, end)
            if end <= last:
                total[s][...] = sums
            else:
                sums = total[s][...] + sums
                for m in range(mats):
                    new = maps_ref[s, m] - step_ref[m] * sums[m * height : (m + 1) * height]
                    maps_new[s][m] = new
                    rounded[s][m] = new.astype(BF16)
    for i in range(last + 1):
        for s in range(own):
            project(rounded[s], column, row, lines_new[i], pl.ds(i * STEP, STEP), every, s)
        if i > 0:
            poisson(i - 1, lines_new[i - 1], every)
    poisson(last, lines_new[last], every)
    stores = []
    for s in range(own):
        groups = [range(mats)] if s < own - 1 else [range(m, m + 1) for m in range(mats)]
        for group in groups:
            sums = back_project(s, 0, last + 1, group)
            for i, m in enumerate(group):
                result[s][m] = maps_new[s][m] - step_ref[m] * sums[i * height : (i + 1) * height]
                copy = pltpu.make_async_copy(result[s].at[m], out_ref.at[m, s], store_sem.at[s, m])
                copy.start()
                stores.append(copy)
    for copy in stores:
        copy.wait()


def solution(mesh):
    n = mesh.shape["view"]

    def local(materials, column_profile, row_profile, start, count, tile_ids, counts, spectrum, attenuation, step):
        mats, own, height, width = materials.shape
        tiles, _, columns = column_profile.shape
        views, bins, window, _ = counts.shape
        energies = spectrum.shape[1]
        assert views == 1 and REACH * own <= ROWS and columns % STEP == 0 and columns > STEP and ITERS == 2
        pairs = own * tiles
        vmem = pl.BlockSpec(memory_space=pltpu.VMEM)
        smem = pl.BlockSpec(memory_space=pltpu.SMEM)
        hbm = pl.BlockSpec(memory_space=pltpu.HBM)
        chunks = columns // STEP
        passed = pl.pallas_call(
            functools.partial(first_kernel, n),
            out_shape=[
                pltpu.VMEM((pairs, mats, columns), F32),
                pltpu.VMEM((REACH, bins + 1, own, columns), F32),
                pltpu.VMEM((own, mats, height, width), F32),
                pltpu.VMEM(column_profile.shape, BF16),
                pltpu.VMEM(row_profile.shape, BF16),
            ],
            in_specs=[hbm] * 7,
            out_specs=[vmem] * 5,
            scratch_shapes=[
                pltpu.VMEM((own, mats, height, width), BF16),
                pltpu.VMEM((bins, window, columns), jnp.int32),
                pltpu.VMEM((2, bins + 1, own, columns), F32),
                pltpu.SMEM((1, 1), jnp.int32),
                pltpu.SMEM((1, 1), jnp.int32),
                pltpu.SMEM(tile_ids.shape, jnp.int32),
                pltpu.SemaphoreType.DMA((own,)),
                pltpu.SemaphoreType.DMA((2, chunks)),
                pltpu.SemaphoreType.DMA,
                pltpu.SemaphoreType.DMA((3,)),
                pltpu.SemaphoreType.DMA((2,)),
                pltpu.SemaphoreType.DMA((2,)),
            ],
            compiler_params=pltpu.CompilerParams(
                collective_id=0, has_side_effects=True, vmem_limit_bytes=24 * 1024 * 1024
            ),
        )(
            start.reshape(1, 1),
            count.reshape(1, 1),
            *[
                pltpu.with_memory_space_constraint(x, pltpu.HBM)
                for x in (tile_ids, materials, column_profile, row_profile, counts)
            ],
        )
        return pl.pallas_call(
            second_kernel,
            out_shape=jax.ShapeDtypeStruct(materials.shape, F32),
            in_specs=[smem] * 3 + [vmem] * 5,
            out_specs=hbm,
            scratch_shapes=[
                [pltpu.VMEM((pairs, mats, STEP), F32)] * chunks,
                [pltpu.VMEM((bins + 1, ROWS, STEP), F32)] * chunks,
                [pltpu.VMEM((pairs, mats, STEP), F32)] * chunks,
                [pltpu.VMEM((mats * height, width), F32)] * own,
                [pltpu.VMEM((mats, height, width), F32)] * own,
                [pltpu.VMEM((mats, height, width), BF16)] * own,
                [pltpu.VMEM((mats, height, width), F32)] * own,
                pltpu.VMEM(((bins + mats) * energies, ROWS, LANES), F32),
                pltpu.SemaphoreType.DMA((own, mats)),
            ],
            compiler_params=pltpu.CompilerParams(vmem_limit_bytes=40 * 1024 * 1024),
        )(spectrum, attenuation.T, step, *passed)

    placed = (
        P(None, ("groups", "view"), None, None),
        P(),
        P(),
        P(("groups", "view")),
        P(("groups", "view")),
        P(("groups", "view"), None),
        P(("groups", "view"), None, None, None),
        P(),
        P(),
        P(),
    )
    return jax.shard_map(
        local,
        mesh=mesh,
        in_specs=placed,
        out_specs=P(None, ("groups", "view"), None, None),
        check_vma=False,
    )
```

```python
import functools

import jax
import jax.numpy as jnp
from jax import lax
from jax.experimental import pallas as pl
from jax.experimental.pallas import tpu as pltpu
from jax.sharding import PartitionSpec as P

ITERS = 2
MESH = pl.DeviceIdType.MESH
F32 = jnp.float32
BF16 = jnp.bfloat16
STEP = 256
LANES = 128
REACH = 3
ROWS = 8
TRANSPOSED = (((1,), (1,)), ((), ()))


def project(block, column, row, lines, cols, to, s):
    mats, height, width = block.shape
    tiles = column.shape[0]
    for t in range(tiles):
        across = jnp.dot(block[...].reshape(mats * height, width), column[t, :, cols], preferred_element_type=F32)
        across = across.reshape(mats, height, cols.size) * row[t, :, cols].astype(F32)[None]
        lines[s * tiles + t, :, to] = jnp.sum(across, axis=1)


def first_kernel(
    n,
    start_hbm,
    count_hbm,
    tiles_hbm,
    mats_ref,
    col_ref,
    row_ref,
    counts_ref,
    lines,
    seen,
    maps,
    column,
    row,
    rounded,
    counts,
    send,
    start_ref,
    count_ref,
    tiles_ref,
    load_sem,
    chunk_sem,
    counts_sem,
    small_sem,
    send_sem,
    recv_sem,
):
    me = lax.axis_index("view")
    mats, own, height, width = mats_ref.shape
    tiles, _, columns = col_ref.shape
    bins, window = counts_ref.shape[1:3]
    has_low, has_high = me > 0, me < n - 1
    low, high = jnp.maximum(me - 1, 0), jnp.minimum(me + 1, n - 1)

    def maps_load(s):
        return pltpu.make_async_copy(mats_ref.at[:, s], maps.at[s], load_sem.at[s])

    def chunk_load(which, i):
        cols = pl.ds(i * STEP, STEP)
        source, target = ((col_ref, column), (row_ref, row))[which]
        return pltpu.make_async_copy(source.at[:, :, cols], target.at[:, :, cols], chunk_sem.at[which, i])

    counts_load = pltpu.make_async_copy(counts_ref.at[0], counts, counts_sem)
    smalls = [
        pltpu.make_async_copy(source, target, small_sem.at[i])
        for i, (source, target) in enumerate(((start_hbm, start_ref), (count_hbm, count_ref), (tiles_hbm, tiles_ref)))
    ]
    for copy in smalls:
        copy.start()
    counts_load.start()
    maps_load(0).start()
    chunk_load(0, 0).start()
    chunk_load(1, 0).start()
    for i in range(1, columns // STEP):
        chunk_load(0, i).start(priority=1)
        chunk_load(1, i).start(priority=1)
    barrier = pltpu.get_barrier_semaphore()

    @pl.when(has_low)
    def _():
        pl.semaphore_signal(barrier, inc=1, device_id={"view": low}, device_id_type=MESH)

    @pl.when(has_high)
    def _():
        pl.semaphore_signal(barrier, inc=1, device_id={"view": high}, device_id_type=MESH)

    nothing = jnp.concatenate([jnp.zeros((bins, own, columns), F32), jnp.full((1, own, columns), -1.0, F32)], axis=0)

    @pl.when(jnp.logical_not(has_low))
    def _():
        seen[0] = nothing

    @pl.when(jnp.logical_not(has_high))
    def _():
        seen[2] = nothing

    def seen_copy(way):
        return pltpu.make_async_remote_copy(
            src_ref=send.at[way],
            dst_ref=seen.at[0 if way == 0 else 2],
            send_sem=send_sem.at[way],
            recv_sem=recv_sem.at[way],
            device_id={"view": high if way == 0 else low},
            device_id_type=MESH,
        )

    sends = ((0, has_high), (1, has_low))
    receives = ((0, has_low), (1, has_high))

    def select():
        for copy in smalls:
            copy.wait()
        counts_load.wait()
        start, number = start_ref[0, 0], count_ref[0, 0]
        for target, shift in ((send.at[0], own), (send.at[1], -own), (seen.at[1], 0)):
            for s in range(own):
                j = me * own + shift + s - start
                held = (j >= 0) & (j < number)
                j = jnp.clip(j, 0, window - 1)
                for e in range(bins):
                    target[e, s : s + 1] = counts[e, pl.ds(j, 1)].astype(F32)
                code = jnp.where(held, tiles_ref[0, j], -1).astype(F32)
                target[bins, s : s + 1] = jnp.full((1, columns), code, F32)

    def exchange():
        pl.semaphore_wait(barrier, has_low.astype(jnp.int32) + has_high.astype(jnp.int32))
        for way, there in sends:

            @pl.when(there)
            def _(way=way):
                seen_copy(way).start()


    select()
    pl.when(me % 2 == 0)(exchange)
    for s in range(own):
        maps_load(s).wait()
        rounded[s] = maps[s].astype(BF16)
        for i in range(columns // STEP):
            if s == 0 and i in (0, 1, 3):
                for j in {0: range(1), 1: range(1, 3), 3: range(3, columns // STEP)}[i]:
                    chunk_load(0, j).wait()
                    chunk_load(1, j).wait()
            project(rounded.at[s], column, row, lines, pl.ds(i * STEP, STEP), pl.ds(i * STEP, STEP), s)
            if s == 0 and i == 0:
                for r in range(1, own):
                    maps_load(r).start(priority=1)
                pl.when(me % 2 == 1)(exchange)

    for way, there in receives:

        @pl.when(there)
        def _(way=way):
            seen_copy(way).wait_recv()

    for way, there in sends:

        @pl.when(there)
        def _(way=way):
            seen_copy(way).wait_send()


def second_kernel(
    spec_ref,
    atten_ref,
    step_ref,
    lines_ref,
    seen_ref,
    maps_ref,
    column,
    row,
    out_ref,
    lines_new,
    counts,
    grad,
    total,
    maps_new,
    rounded,
    result,
    table,
    store_sem,
):
    own, mats, height, width = maps_ref.shape
    tiles, _, columns = column.shape
    bins, energies = spec_ref.shape
    last = columns // STEP - 1

    atten_at = bins * energies
    for e in range(bins):
        for k in range(energies):
            table[e * energies + k] = jnp.full((ROWS, LANES), spec_ref[e, k], F32)
    for m in range(mats):
        for k in range(energies):
            table[atten_at + m * energies + k] = jnp.full((ROWS, LANES), atten_ref[m, k], F32)

    def fixed(at):
        return jnp.concatenate([table[at]] * (STEP // LANES), axis=1)

    def held_by(i):
        code = counts[i][bins]
        slot = lax.broadcasted_iota(jnp.int32, code.shape, 0) % own
        return [(code == t) & (slot == s) for s in range(own) for t in range(tiles)]

    def gather(i):
        cols = pl.ds(i * STEP, STEP)
        empty = jnp.zeros((ROWS - REACH * own, STEP), F32)
        for e in range(bins + 1):
            fill = empty if e < bins else empty - 1.0
            counts[i][e] = jnp.concatenate([seen_ref[w, e, :, cols] for w in range(REACH)] + [fill], axis=0)

    def poisson(i, lines, cols):
        held = held_by(i)
        xs = []
        for m in range(mats):
            x = jnp.zeros((ROWS, STEP), F32)
            for p in range(own * tiles):
                x = jnp.where(held[p], lines[p, m : m + 1, cols], x)
            xs.append(x)
        trans = []
        for k in range(energies):
            exponent = fixed(atten_at + k) * xs[0]
            for m in range(1, mats):
                exponent = exponent + fixed(atten_at + m * energies + k) * xs[m]
            trans.append(jnp.exp(-exponent))
        back = [None] * energies
        for e in range(bins):
            expected = fixed(e * energies) * trans[0]
            for k in range(1, energies):
                expected = expected + fixed(e * energies + k) * trans[k]
            weight = 1.0 - counts[i][e] / expected
            for k in range(energies):
                term = fixed(e * energies + k) * weight
                back[k] = term if e == 0 else back[k] + term
        for m in range(mats):
            slope = None
            for k in range(energies):
                term = fixed(atten_at + m * energies + k) * (trans[k] * back[k])
                slope = term if k == 0 else slope + term
            slope = (-slope).astype(BF16).astype(F32)
            for p in range(own * tiles):
                grad[i][p, m : m + 1] = jnp.sum(jnp.where(held[p], slope, 0.0), axis=0, keepdims=True)

    def back_project(s, first, end, group=None):
        sums = None
        for t in range(tiles):
            blocks = []
            for i in range(first, end):
                g = grad[i][s * tiles + t]
                profile = row[t, :, i * STEP : (i + 1) * STEP].astype(F32)
                blocks.append(
                    jnp.concatenate([(g[m : m + 1] * profile).astype(BF16) for m in group or range(mats)], axis=0)
                )
            weighted = jnp.concatenate(blocks, axis=1)
            part = lax.dot_general(
                weighted, column[t, :, first * STEP : end * STEP], TRANSPOSED, preferred_element_type=F32
            )
            sums = part if t == 0 else sums + part
        return sums

    every = pl.ds(0, STEP)
    gather(0)
    poisson(0, lines_ref, every)
    for first, end in ((0, 1), (1, last + 1)):
        if first == 0:
            for i in range(end, last + 1):
                gather(i)
                poisson(i, lines_ref, pl.ds(i * STEP, STEP))
        for s in range(own):
            sums = back_project(s, first, end)
            if end <= last:
                total[s][...] = sums
            else:
                sums = total[s][...] + sums
                for m in range(mats):
                    new = maps_ref[s, m] - step_ref[m] * sums[m * height : (m + 1) * height]
                    maps_new[s][m] = new
                    rounded[s][m] = new.astype(BF16)
    for i in range(last + 1):
        for s in range(own):
            project(rounded[s], column, row, lines_new[i], pl.ds(i * STEP, STEP), every, s)
        if i > 0:
            poisson(i - 1, lines_new[i - 1], every)
    poisson(last, lines_new[last], every)
    stores = []
    for s in range(own):
        groups = [range(mats)] if s < own - 1 else [range(m, m + 1) for m in range(mats)]
        for group in groups:
            sums = back_project(s, 0, last + 1, group)
            for i, m in enumerate(group):
                result[s][m] = maps_new[s][m] - step_ref[m] * sums[i * height : (i + 1) * height]
                copy = pltpu.make_async_copy(result[s].at[m], out_ref.at[m, s], store_sem.at[s, m])
                copy.start()
                stores.append(copy)
    for copy in stores:
        copy.wait()


def solution(mesh):
    n = mesh.shape["view"]

    def local(materials, column_profile, row_profile, start, count, tile_ids, counts, spectrum, attenuation, step):
        mats, own, height, width = materials.shape
        tiles, _, columns = column_profile.shape
        views, bins, window, _ = counts.shape
        energies = spectrum.shape[1]
        assert views == 1 and REACH * own <= ROWS and columns % STEP == 0 and columns > STEP and ITERS == 2
        pairs = own * tiles
        vmem = pl.BlockSpec(memory_space=pltpu.VMEM)
        smem = pl.BlockSpec(memory_space=pltpu.SMEM)
        hbm = pl.BlockSpec(memory_space=pltpu.HBM)
        chunks = columns // STEP
        passed = pl.pallas_call(
            functools.partial(first_kernel, n),
            out_shape=[
                pltpu.VMEM((pairs, mats, columns), F32),
                pltpu.VMEM((REACH, bins + 1, own, columns), F32),
                pltpu.VMEM((own, mats, height, width), F32),
                pltpu.VMEM(column_profile.shape, BF16),
                pltpu.VMEM(row_profile.shape, BF16),
            ],
            in_specs=[hbm] * 7,
            out_specs=[vmem] * 5,
            scratch_shapes=[
                pltpu.VMEM((own, mats, height, width), BF16),
                pltpu.VMEM((bins, window, columns), jnp.int32),
                pltpu.VMEM((2, bins + 1, own, columns), F32),
                pltpu.SMEM((1, 1), jnp.int32),
                pltpu.SMEM((1, 1), jnp.int32),
                pltpu.SMEM(tile_ids.shape, jnp.int32),
                pltpu.SemaphoreType.DMA((own,)),
                pltpu.SemaphoreType.DMA((2, chunks)),
                pltpu.SemaphoreType.DMA,
                pltpu.SemaphoreType.DMA((3,)),
                pltpu.SemaphoreType.DMA((2,)),
                pltpu.SemaphoreType.DMA((2,)),
            ],
            compiler_params=pltpu.CompilerParams(
                collective_id=0, has_side_effects=True, vmem_limit_bytes=24 * 1024 * 1024
            ),
        )(
            start.reshape(1, 1),
            count.reshape(1, 1),
            *[
                pltpu.with_memory_space_constraint(x, pltpu.HBM)
                for x in (tile_ids, materials, column_profile, row_profile, counts)
            ],
        )
        return pl.pallas_call(
            second_kernel,
            out_shape=jax.ShapeDtypeStruct(materials.shape, F32),
            in_specs=[smem] * 3 + [vmem] * 5,
            out_specs=hbm,
            scratch_shapes=[
                [pltpu.VMEM((pairs, mats, STEP), F32)] * chunks,
                [pltpu.VMEM((bins + 1, ROWS, STEP), F32)] * chunks,
                [pltpu.VMEM((pairs, mats, STEP), F32)] * chunks,
                [pltpu.VMEM((mats * height, width), F32)] * own,
                [pltpu.VMEM((mats, height, width), F32)] * own,
                [pltpu.VMEM((mats, height, width), BF16)] * own,
                [pltpu.VMEM((mats, height, width), F32)] * own,
                pltpu.VMEM(((bins + mats) * energies, ROWS, LANES), F32),
                pltpu.SemaphoreType.DMA((own, mats)),
            ],
            compiler_params=pltpu.CompilerParams(vmem_limit_bytes=40 * 1024 * 1024),
        )(spectrum, attenuation.T, step, *passed)

    placed = (
        P(None, ("groups", "view"), None, None),
        P(),
        P(),
        P(("groups", "view")),
        P(("groups", "view")),
        P(("groups", "view"), None),
        P(("groups", "view"), None, None, None),
        P(),
        P(),
        P(),
    )
    return jax.shard_map(
        local,
        mesh=mesh,
        in_specs=placed,
        out_specs=P(None, ("groups", "view"), None, None),
        check_vma=False,
    )
```
